32 devices in a mesh: space: 4 (over x, core), mem: 8 (over z, y).
Axes of the slice: x: 2, y: 2, z: 4, core: 2. Of those that a mesh axis runs over, the one named last changes fastest.
Arguments:
- prior_ensemble: float32 [512, 8192], P('mem', 'space'), may hold values from -5 to 5
- terminal_particles: float32 [512, 8192], P(None, ('space', 'mem')), may hold values from -5 to 5
- reverse_perturbation: float32 [3, 512, 8192], P(None, None, ('space', 'mem')), may hold values from -6 to 6
- measured_angles: float32 [8192], P(('space', 'mem')), may hold values from -1.3 to 1.3
Outputs:
- analysis: float32 [512, 8192], P(None, ('space', 'mem'))
The draws below stay inside these ranges and needn't reach their ends.
All inputs are finite; a program needn't handle non-finite values.
Results may differ from the reference program's by a relative error of at most 0.0003.
Values sent between devices are 32-bit elements; how exact they have to be, the bound alone decides.
A program may use at most 64 MiB of HBM per device.

```python
import math
import jax
import jax.numpy as jnp
from jax import lax

M = 512
S = 512
ITERS = 3
V = 8192


def member_field(key):
    base = jax.random.fold_in(key, 7)
    first = jax.random.fold_in(base, 0)
    return jnp.clip(jax.random.normal(first, (M, V), jnp.float32), -5.0, 5.0)


def draw_prior_ensemble(key, part):
    return member_field(key).astype(jnp.float32)


def draw_terminal_particles(key, part):
    base = jax.random.fold_in(key, 11)
    return jnp.clip(jax.random.normal(base, (S, V), jnp.float32), -5.0, 5.0)


def block_levels(rng, extent, pieces, low, largest):
    def one(position, shards_of):
        steps = jax.random.uniform(jax.random.fold_in(jax.random.fold_in(rng, 6), position), (shards_of,), jnp.float32, low / len(pieces), largest / len(pieces))
        return jnp.repeat(jnp.exp(steps), extent[position] // shards_of).reshape((-1,) + (1,) * (len(extent) - position - 1))

    factor_of = one(*pieces[0])
    for cut in pieces[1:]:
        factor_of = factor_of * one(*cut)
    return factor_of


def noise(key, shape, scale, reach, pieces=(), kind=jnp.bfloat16):
    array = scale * jax.random.normal(key, shape, jnp.float32)
    if pieces:
        array = array * block_levels(key, shape, pieces, -0.22, 0.18)
    return jnp.clip(array, -reach, reach).astype(kind)


def setup_inputs(seed: int = 0) -> dict:
    key_list = jax.random.split(jax.random.key(seed), 5)
    prior_ensemble = draw_prior_ensemble(jax.random.fold_in(key_list[4], 71), 0)
    terminal_particles = draw_terminal_particles(jax.random.fold_in(key_list[4], 71), 0)
    reverse_perturbation = noise(key_list[2], (ITERS, S, V), 1.0, 6.0, ((2, 32),), jnp.float32)
    measured_angles = jnp.clip(jax.random.uniform(key_list[3], (V,), jnp.float32, -1.3, 1.3) * block_levels(key_list[3], (V,), ((0, 32),), -0.4, 0.0), -1.3, 1.3)
    return {"prior_ensemble": prior_ensemble, "terminal_particles": terminal_particles, "reverse_perturbation": reverse_perturbation, "measured_angles": measured_angles}


def reference(prior_ensemble, terminal_particles, reverse_perturbation, measured_angles):
    peak_log_likelihood = lax.Precision.HIGHEST
    particle_lengths = lax.optimization_barrier(jnp.sum(prior_ensemble * prior_ensemble, axis=1))
    temper = math.sqrt(V)
    gaussian_variates = terminal_particles
    for step in range(ITERS):
        t = 1.0 - step / ITERS
        dt = 1.0 / ITERS
        alpha = 1.0 - 0.5 * t
        sigma2 = t
        drift = -0.5 / alpha
        g2 = 1.0 + t / alpha
        damp = 1.0 - t
        inner_pairing_matrix = jnp.dot(gaussian_variates, prior_ensemble.T, precision=peak_log_likelihood, preferred_element_type=jnp.float32)
        logits = (2.0 * alpha * inner_pairing_matrix - alpha * alpha * particle_lengths[None, :]) / (2.0 * sigma2 * temper)
        annealed_importance = jax.nn.softmax(logits, axis=1)
        mixed_correction = jnp.dot(annealed_importance, prior_ensemble, precision=peak_log_likelihood, preferred_element_type=jnp.float32)
        score = -(gaussian_variates - alpha * mixed_correction) / sigma2 + damp * 4.0 * (measured_angles[None, :] - jnp.arctan(gaussian_variates)) / (1.0 + gaussian_variates * gaussian_variates)
        gaussian_variates = gaussian_variates + dt * (-drift * gaussian_variates + g2 * score) + math.sqrt(dt * g2) * reverse_perturbation[step]
    return gaussian_variates
```

```python
import functools
import math

import jax
import jax.numpy as jnp
from jax import lax
from jax.experimental import pallas as pl
from jax.experimental.pallas import tpu as pltpu
from jax.sharding import PartitionSpec as P

ITERS = 3
CHUNKS = 2
CORES = 2
SUBLANES = 8
MESH = pl.DeviceIdType.MESH
HIGHEST = lax.Precision.HIGHEST


def dot(a, b, contract_b):
    return lax.dot_general(
        a,
        b,
        (((1,), (contract_b,)), ((), ())),
        precision=HIGHEST,
        preferred_element_type=jnp.float32,
    )


def arctan(x):
    a = jnp.abs(x)
    big = a > 2.414213562373095
    mid = a > 0.4142135623730950
    num = jnp.where(big, -1.0, jnp.where(mid, a - 1.0, a))
    den = jnp.where(big, a, jnp.where(mid, a + 1.0, 1.0))
    base = jnp.where(big, math.pi / 2, jnp.where(mid, math.pi / 4, 0.0))
    r = num / den
    s = r * r
    poly = ((8.05374449538e-2 * s - 1.38776856032e-1) * s + 1.99777106478e-1) * s
    poly = (poly - 3.33329491539e-1) * s * r + r
    y = base + poly
    return jnp.where(x < 0.0, -y, y)


def rows_at(start, size):
    return pl.ds(pl.multiple_of(start, SUBLANES), size)


def kernel(
    plan,
    prior,
    terminal,
    perturbation,
    angles,
    out,
    x,
    z,
    noise,
    give,
    keep,
    core_in,
    xy_in,
    part,
    z_in,
    w,
    send,
    recv,
    xsend,
    xrecv,
    local,
    osem,
):
    n_space, n_mem, ny, nz, scatter_z, temper = plan
    nxy = (n_space // CORES) * ny
    rows = z.shape[0] // CHUNKS
    rows2 = rows // CORES
    rows3 = rows2 // nxy
    rows4 = rows3 // nz if scatter_z else rows3
    members = prior.shape[0]
    variables = x.shape[1]

    sp = lax.axis_index("space")
    me = lax.axis_index("mem")
    core = lax.rem(sp, CORES)
    other = 1 - core
    xi = lax.div(sp, CORES)
    yi = lax.rem(me, ny)
    zi = lax.div(me, ny)
    q = xi * ny + yi

    core_dev = (xi * CORES + other, me)

    def xy_peer(d):
        p = lax.rem(q + d, nxy)
        return p, (lax.div(p, ny) * CORES + core, zi * ny + lax.rem(p, ny))

    def z_peer(d):
        p = lax.rem(zi + d, nz)
        return p, (sp, p * ny + yi)

    def mem_peer(d):
        p = lax.rem(me + d, n_mem)
        return p, (sp, p)

    def cols(p):
        return pl.ds(pl.multiple_of(p * variables, variables), variables)

    loads = [
        pltpu.make_async_copy(terminal, z, local.at[0]),
        pltpu.make_async_copy(perturbation, noise, local.at[1]),
        pltpu.make_async_copy(
            prior.at[:, cols(me)], x.at[rows_at(me * members, members), :], local.at[2]
        ),
    ]
    for copy in loads:
        copy.start()

    barrier = pltpu.get_barrier_semaphore()
    greet = [core_dev]
    greet += [xy_peer(d)[1] for d in range(1, nxy)]
    greet += [mem_peer(d)[1] for d in range(1, n_mem)]
    for dev in greet:
        pl.semaphore_signal(barrier, inc=1, device_id=dev, device_id_type=MESH)
    pl.semaphore_wait(barrier, len(greet))

    exchange = []
    for d in range(1, n_mem):
        p, dev = mem_peer(d)
        exchange.append(
            pltpu.make_async_remote_copy(
                src_ref=prior.at[:, cols(p)],
                dst_ref=x.at[rows_at(me * members, members), :],
                send_sem=xsend.at[d - 1],
                recv_sem=xrecv.at[d - 1],
                device_id=dev,
                device_id_type=MESH,
            )
        )
        exchange[-1].start()
    for copy in loads:
        copy.wait()
    for copy in exchange:
        copy.wait_recv()

    xs = x[...]
    norms = dot(jnp.ones((SUBLANES, variables), jnp.float32), xs * xs, 1)[:1]

    first_xy = 1
    first_z = first_xy + nxy - 1
    first_gz = first_z + nz - 1
    first_gxy = first_gz + nz - 1
    last_core = first_gxy + nxy - 1

    def chunk(c):
        base = c * rows
        for k in range(ITERS):
            t = 1.0 - k / ITERS
            dt = 1.0 / ITERS
            alpha = 1.0 - 0.5 * t
            drift = -0.5 / alpha
            g2 = 1.0 + t / alpha
            damp = 1.0 - t
            started = []

            def put(src, dst, i, dev):
                copy = pltpu.make_async_remote_copy(
                    src_ref=src,
                    dst_ref=dst,
                    send_sem=send.at[k % 2, c, i],
                    recv_sem=recv.at[k % 2, c, i],
                    device_id=dev,
                    device_id_type=MESH,
                )
                copy.start()
                started.append(copy)
                return copy

            def numerator(half):
                zs = z[rows_at(base + half * rows2, rows2), :]
                return 2.0 * alpha * dot(zs, x[...], 1) - alpha * alpha * norms

            give[c] = numerator(other)
            swap = put(give.at[c], core_in.at[c], 0, core_dev)
            keep[c] = numerator(core)
            yield
            swap.wait_recv()
            group = []
            for d in range(1, nxy):
                p, dev = xy_peer(d)
                block = rows_at(p * rows3, rows3)
                keep[c, block, :] = keep[c, block, :] + core_in[c, block, :]
                group.append(put(keep.at[c, block, :], xy_in.at[c, d - 1], first_xy + d - 1, dev))
            block = rows_at(q * rows3, rows3)
            total = keep[c, block, :] + core_in[c, block, :]
            yield
            for d, copy in enumerate(group):
                copy.wait_recv()
                total = total + xy_in[c, d]
            part[c] = total
            group = []
            for d in range(1, nz):
                p, dev = z_peer(d)
                src = part.at[c, rows_at(p * rows4, rows4), :] if scatter_z else part.at[c]
                group.append(put(src, z_in.at[k % 2, c, d - 1], first_z + d - 1, dev))
            total = part[c, rows_at(zi * rows4, rows4), :] if scatter_z else total
            yield
            for d, copy in enumerate(group):
                copy.wait_recv()
                total = total + z_in[k % 2, c, d]
            logits = total / (2.0 * t * temper)
            e = jnp.exp(logits - jnp.max(logits, axis=1, keepdims=True))
            weights = e / jnp.sum(e, axis=1, keepdims=True)
            mine = core * rows2 + q * rows3
            if scatter_z:
                block = rows_at(mine + zi * rows4, rows4)
                w[c, block, :] = weights
                group = [
                    put(w.at[c, block, :], w.at[c, block, :], first_gz + d - 1, z_peer(d)[1])
                    for d in range(1, nz)
                ]
                yield
                for copy in group:
                    copy.wait_recv()
            else:
                w[c, rows_at(mine, rows3), :] = weights
            block = rows_at(mine, rows3)
            group = [
                put(w.at[c, block, :], w.at[c, block, :], first_gxy + d - 1, xy_peer(d)[1])
                for d in range(1, nxy)
            ]
            yield
            for copy in group:
                copy.wait_recv()
            half = rows_at(core * rows2, rows2)
            swap = put(w.at[c, half, :], w.at[c, half, :], last_core, core_dev)

            def advance(half):
                where = rows_at(base + half * rows2, rows2)
                blend = dot(w[c, rows_at(half * rows2, rows2), :], x[...], 0)
                zs = z[where, :]
                score = -(zs - alpha * blend) / t + damp * 4.0 * (
                    angles[...] - arctan(zs)
                ) / (1.0 + zs * zs)
                z[where, :] = (
                    zs
                    + dt * (-drift * zs + g2 * score)
                    + math.sqrt(dt * g2) * noise[k, where, :]
                )

            advance(core)
            yield
            swap.wait_recv()
            advance(other)
            for copy in started:
                copy.wait_send()
        result = pltpu.make_async_copy(
            z.at[pl.ds(base, rows), :], out.at[pl.ds(base, rows), :], osem.at[c]
        )
        result.start()
        yield
        result.wait()

    running = [chunk(c) for c in range(CHUNKS)]
    while running:
        still = []
        for item in running:
            try:
                next(item)
                still.append(item)
            except StopIteration:
                pass
        running = still
    for copy in exchange:
        copy.wait_send()


def per_device(prior, terminal, perturbation, angles):
    n_space, n_mem = lax.axis_size("space"), lax.axis_size("mem")
    samples, variables = terminal.shape
    members = prior.shape[0] * n_mem
    nx = n_space // CORES
    ny = math.gcd(nx, n_mem)
    nz = n_mem // ny
    nxy = nx * ny
    rows = samples // CHUNKS
    rows2 = rows // CORES
    rows3 = rows2 // nxy
    scatter_z = rows3 % (nz * SUBLANES) == 0
    rows4 = rows3 // nz if scatter_z else rows3
    temper = math.sqrt(variables * n_space * n_mem)
    f32 = jnp.float32
    exchanges = 2 * (1 + nxy - 1 + nz - 1)
    iters = perturbation.shape[0]
    anywhere = pl.BlockSpec(memory_space=pl.ANY)
    return pl.pallas_call(
        functools.partial(kernel, (n_space, n_mem, ny, nz, scatter_z, temper)),
        out_shape=jax.ShapeDtypeStruct((samples, variables), f32),
        in_specs=[anywhere] * 3 + [pl.BlockSpec(memory_space=pltpu.VMEM)],
        out_specs=anywhere,
        scratch_shapes=[
            pltpu.VMEM((members, variables), f32),
            pltpu.VMEM((samples, variables), f32),
            pltpu.VMEM((iters, samples, variables), f32),
            pltpu.VMEM((CHUNKS, rows2, members), f32),
            pltpu.VMEM((CHUNKS, rows2, members), f32),
            pltpu.VMEM((CHUNKS, rows2, members), f32),
            pltpu.VMEM((CHUNKS, nxy - 1, rows3, members), f32),
            pltpu.VMEM((CHUNKS, rows3, members), f32),
            pltpu.VMEM((2, CHUNKS, nz - 1, rows4, members), f32),
            pltpu.VMEM((CHUNKS, rows, members), f32),
            pltpu.SemaphoreType.DMA((2, CHUNKS, exchanges)),
            pltpu.SemaphoreType.DMA((2, CHUNKS, exchanges)),
            pltpu.SemaphoreType.DMA((n_mem - 1,)),
            pltpu.SemaphoreType.DMA((n_mem - 1,)),
            pltpu.SemaphoreType.DMA((3,)),
            pltpu.SemaphoreType.DMA((CHUNKS,)),
        ],
        compiler_params=pltpu.CompilerParams(collective_id=0, has_side_effects=True),
    )(prior, terminal, perturbation, angles.reshape(1, variables))


def solution(mesh):
    in_specs = (
        P("mem", "space"),
        P(None, ("space", "mem")),
        P(None, None, ("space", "mem")),
        P(("space", "mem")),
    )
    out_specs = P(None, ("space", "mem"))
    return jax.shard_map(
        per_device, mesh=mesh, in_specs=in_specs, out_specs=out_specs, check_vma=False
    )
```

```python
import functools
import math

import jax
import jax.numpy as jnp
from jax import lax
from jax.experimental import pallas as pl
from jax.experimental.pallas import tpu as pltpu
from jax.sharding import PartitionSpec as P

ITERS = 3
CHUNKS = 4
CORES = 2
SUBLANES = 8
LANES = 128
MESH = pl.DeviceIdType.MESH
HIGHEST = lax.Precision.HIGHEST


def dot(a, b, contract_b):
    return lax.dot_general(
        a,
        b,
        (((1,), (contract_b,)), ((), ())),
        precision=HIGHEST,
        preferred_element_type=jnp.float32,
    )


def arctan(x):
    a = jnp.abs(x)
    big = a > 2.414213562373095
    mid = a > 0.4142135623730950
    num = jnp.where(big, -1.0, jnp.where(mid, a - 1.0, a))
    den = jnp.where(big, a, jnp.where(mid, a + 1.0, 1.0))
    base = jnp.where(big, math.pi / 2, jnp.where(mid, math.pi / 4, 0.0))
    r = num / den
    s = r * r
    poly = ((8.05374449538e-2 * s - 1.38776856032e-1) * s + 1.99777106478e-1) * s
    poly = (poly - 3.33329491539e-1) * s * r + r
    y = base + poly
    return jnp.where(x < 0.0, -y, y)


def rows_at(start, size):
    return pl.ds(pl.multiple_of(start, SUBLANES), size)


def kernel(
    plan,
    prior,
    terminal,
    perturbation,
    angles,
    out,
    x,
    z,
    noise,
    seen,
    gram,
    xy_in,
    part,
    z_in,
    numer,
    w,
    send,
    recv,
    once_send,
    once_recv,
    local,
):
    n_space, n_mem, ny, nz, scatter_z, temper = plan
    nxy = (n_space // CORES) * ny
    chunks, rows, _ = gram.shape
    rows3 = rows // nxy
    samples = z.shape[0]
    members = prior.shape[0]
    variables = terminal.shape[1]
    lanes = numer.shape[3]

    sp = lax.axis_index("space")
    me = lax.axis_index("mem")
    core = lax.rem(sp, CORES)
    other = 1 - core
    xi = lax.div(sp, CORES)
    yi = lax.rem(me, ny)
    zi = lax.div(me, ny)
    q = xi * ny + yi

    core_dev = (xi * CORES + other, me)

    def xy_peer(d):
        p = lax.rem(q + d, nxy)
        return p, (lax.div(p, ny) * CORES + core, zi * ny + lax.rem(p, ny))

    def z_peer(d):
        p = lax.rem(zi + d, nz)
        return p, (sp, p * ny + yi)

    def mem_peer(d):
        p = lax.rem(me + d, n_mem)
        return p, (sp, p)

    def cols(p):
        return pl.ds(pl.multiple_of(p * variables, variables), variables)

    mine = cols(core)
    my_samples = rows_at(core * samples, samples)
    its_samples = rows_at(other * samples, samples)
    my_members = rows_at(me * members, members)

    loads = [
        pltpu.make_async_copy(
            prior.at[:, cols(me)], x.at[my_members, mine], local.at[0]
        ),
        pltpu.make_async_copy(terminal.at[my_samples, :], z.at[:, mine], local.at[1]),
        pltpu.make_async_copy(angles, seen.at[:, mine], local.at[2]),
        pltpu.make_async_copy(
            perturbation.at[:, my_samples, :], noise.at[:, :, mine], local.at[3]
        ),
    ]
    for copy in loads:
        copy.start()

    barrier = pltpu.get_barrier_semaphore()
    greet = [core_dev]
    greet += [xy_peer(d)[1] for d in range(1, nxy)]
    greet += [mem_peer(d)[1] for d in range(1, n_mem)]
    for dev in greet:
        pl.semaphore_signal(barrier, inc=1, device_id=dev, device_id_type=MESH)
    pl.semaphore_wait(barrier, len(greet))

    def put_once(src, dst, i, dev):
        copy = pltpu.make_async_remote_copy(
            src_ref=src,
            dst_ref=dst,
            send_sem=once_send.at[i],
            recv_sem=once_recv.at[i],
            device_id=dev,
            device_id_type=MESH,
        )
        copy.start()
        return copy

    exchange = []
    for d in range(1, n_mem):
        p, dev = mem_peer(d)
        exchange.append(put_once(prior.at[:, cols(p)], x.at[my_members, mine], d - 1, dev))
    i = n_mem - 1
    swaps = [
        put_once(terminal.at[its_samples, :], z.at[:, mine], i, core_dev),
        put_once(angles, seen.at[:, mine], i + 1, core_dev),
        put_once(prior.at[:, cols(me)], x.at[my_members, mine], i + 2, core_dev),
        put_once(perturbation.at[:, its_samples, :], noise.at[:, :, mine], i + 3, core_dev),
    ]
    i = i + 4
    for d, copy in enumerate(exchange):
        copy.wait_recv()
        theirs = rows_at(lax.rem(me + n_mem - d - 1, n_mem) * members, members)
        swaps.append(put_once(x.at[theirs, mine], x.at[theirs, mine], i + d, core_dev))
    i = i + n_mem - 1
    for copy in loads:
        copy.wait()
    for copy in swaps:
        copy.wait_recv()

    xs = x[...]
    norms = dot(jnp.ones((SUBLANES, xs.shape[1]), jnp.float32), xs * xs, 1)[:1]

    first_z = nxy - 1
    first_gz = first_z + nz - 1
    first_gxy = first_gz + nz - 1

    def chunk(c):
        where = pl.ds(c * rows, rows)
        mine_xy = rows_at(q * rows3, rows3)
        for k in range(ITERS):
            t = 1.0 - k / ITERS
            dt = 1.0 / ITERS
            alpha = 1.0 - 0.5 * t
            drift = -0.5 / alpha
            g2 = 1.0 + t / alpha
            damp = 1.0 - t
            started = []

            def put(src, dst, i, dev):
                copy = pltpu.make_async_remote_copy(
                    src_ref=src,
                    dst_ref=dst,
                    send_sem=send.at[k % 2, c, i],
                    recv_sem=recv.at[k % 2, c, i],
                    device_id=dev,
                    device_id_type=MESH,
                )
                copy.start()
                started.append(copy)
                return copy

            gram[c] = 2.0 * alpha * dot(z[where, :], x[...], 1) - alpha * alpha * norms
            group = []
            for d in range(1, nxy):
                p, dev = xy_peer(d)
                group.append(
                    put(gram.at[c, rows_at(p * rows3, rows3), :], xy_in.at[c, d - 1], d - 1, dev)
                )
            yield
            total = gram[c, mine_xy, :]
            for d, copy in enumerate(group):
                copy.wait_recv()
                total = total + xy_in[c, d]
            group = []
            if scatter_z:
                for p in range(nz):
                    part[c, p] = total[:, p * lanes : (p + 1) * lanes]
            else:
                part[c, 0] = total
            for d in range(1, nz):
                p, dev = z_peer(d)
                src = part.at[c, p] if scatter_z else part.at[c, 0]
                group.append(put(src, z_in.at[k % 2, c, d - 1], first_z + d - 1, dev))
            yield
            block = part[c, zi] if scatter_z else part[c, 0]
            for d, copy in enumerate(group):
                copy.wait_recv()
                block = block + z_in[k % 2, c, d]
            if scatter_z:
                numer[c, zi] = block
                group = [
                    put(numer.at[c, zi], numer.at[c, zi], first_gz + d - 1, z_peer(d)[1])
                    for d in range(1, nz)
                ]
                yield
                for copy in group:
                    copy.wait_recv()
                block = jnp.concatenate([numer[c, p] for p in range(nz)], axis=1)
            logits = block / (2.0 * t * temper)
            e = jnp.exp(logits - jnp.max(logits, axis=1, keepdims=True))
            w[c, mine_xy, :] = e / jnp.sum(e, axis=1, keepdims=True)
            group = [
                put(w.at[c, mine_xy, :], w.at[c, mine_xy, :], first_gxy + d - 1, xy_peer(d)[1])
                for d in range(1, nxy)
            ]
            yield
            for copy in group:
                copy.wait_recv()
            blend = dot(w[c], x[...], 0)
            zs = z[where, :]
            score = -(zs - alpha * blend) / t + damp * 4.0 * (seen[...] - arctan(zs)) / (
                1.0 + zs * zs
            )
            z[where, :] = (
                zs + dt * (-drift * zs + g2 * score) + math.sqrt(dt * g2) * noise[k, where, :]
            )
            for copy in started:
                copy.wait_send()
        target = out.at[rows_at(core * samples + c * rows, rows), :]
        result = pltpu.make_async_copy(z.at[where, mine], target, local.at[4 + c])
        result.start()
        swap = put_once(z.at[where, cols(other)], target, i + c, core_dev)
        yield
        result.wait()
        swap.wait()

    running = [chunk(c) for c in range(chunks)]
    while running:
        still = []
        for item in running:
            try:
                next(item)
                still.append(item)
            except StopIteration:
                pass
        running = still
    for copy in exchange + swaps:
        copy.wait_send()


def per_device(prior, terminal, perturbation, angles):
    n_space, n_mem = lax.axis_size("space"), lax.axis_size("mem")
    samples, variables = terminal.shape
    members = prior.shape[0] * n_mem
    nx = n_space // CORES
    ny = math.gcd(nx, n_mem)
    nz = n_mem // ny
    nxy = nx * ny
    half = samples // CORES
    chunks = CHUNKS
    while chunks > 1 and half % (chunks * nxy * SUBLANES):
        chunks //= 2
    rows = half // chunks
    rows3 = rows // nxy
    scatter_z = members % (nz * LANES) == 0
    pieces = nz if scatter_z else 1
    lanes = members // pieces
    temper = math.sqrt(variables * n_space * n_mem)
    f32 = jnp.float32
    exchanges = 2 * (nxy - 1 + nz - 1)
    once = 2 * (n_mem - 1) + 4 + chunks
    iters = perturbation.shape[0]
    anywhere = pl.BlockSpec(memory_space=pl.ANY)
    return pl.pallas_call(
        functools.partial(kernel, (n_space, n_mem, ny, nz, scatter_z, temper)),
        out_shape=jax.ShapeDtypeStruct((samples, variables), f32),
        in_specs=[anywhere] * 4,
        out_specs=anywhere,
        scratch_shapes=[
            pltpu.VMEM((members, CORES * variables), f32),
            pltpu.VMEM((half, CORES * variables), f32),
            pltpu.VMEM((iters, half, CORES * variables), f32),
            pltpu.VMEM((1, CORES * variables), f32),
            pltpu.VMEM((chunks, rows, members), f32),
            pltpu.VMEM((chunks, nxy - 1, rows3, members), f32),
            pltpu.VMEM((chunks, pieces, rows3, lanes), f32),
            pltpu.VMEM((2, chunks, nz - 1, rows3, lanes), f32),
            pltpu.VMEM((chunks, pieces, rows3, lanes), f32),
            pltpu.VMEM((chunks, rows, members), f32),
            pltpu.SemaphoreType.DMA((2, chunks, exchanges)),
            pltpu.SemaphoreType.DMA((2, chunks, exchanges)),
            pltpu.SemaphoreType.DMA((once,)),
            pltpu.SemaphoreType.DMA((once,)),
            pltpu.SemaphoreType.DMA((4 + chunks,)),
        ],
        compiler_params=pltpu.CompilerParams(collective_id=0, has_side_effects=True),
    )(prior, terminal, perturbation, angles.reshape(1, variables))


def solution(mesh):
    in_specs = (
        P("mem", "space"),
        P(None, ("space", "mem")),
        P(None, None, ("space", "mem")),
        P(("space", "mem")),
    )
    out_specs = P(None, ("space", "mem"))
    return jax.shard_map(
        per_device, mesh=mesh, in_specs=in_specs, out_specs=out_specs, check_vma=False
    )
```

```python
import functools
import math

import jax
import jax.numpy as jnp
from jax import lax
from jax.experimental import pallas as pl
from jax.experimental.pallas import tpu as pltpu
from jax.sharding import PartitionSpec as P

ITERS = 3
CHUNKS = 4
CORES = 2
SUBLANES = 8
LANES = 128
MESH = pl.DeviceIdType.MESH


def split(a, parts):
    out = []
    for _ in range(parts):
        out.append(a.astype(jnp.bfloat16))
        a = a - out[-1].astype(jnp.float32)
    return out


def product(a, parts, contract_b):
    n = a.shape[0]
    lhs = split(a, len(parts))
    total = None
    for i in reversed(range(len(parts))):
        rows = lhs[: len(parts) - i]
        both = lax.dot_general(
            jnp.concatenate(rows, axis=0),
            parts[i],
            (((1,), (contract_b,)), ((), ())),
            preferred_element_type=jnp.float32,
        )
        for j in reversed(range(len(rows))):
            term = both[j * n : (j + 1) * n]
            total = term if total is None else total + term
    return total


def arctan(x):
    a = jnp.abs(x)
    big = a > 2.414213562373095
    mid = a > 0.4142135623730950
    num = jnp.where(big, -1.0, jnp.where(mid, a - 1.0, a))
    den = jnp.where(big, a, jnp.where(mid, a + 1.0, 1.0))
    base = jnp.where(big, math.pi / 2, jnp.where(mid, math.pi / 4, 0.0))
    r = num / den
    s = r * r
    poly = ((8.05374449538e-2 * s - 1.38776856032e-1) * s + 1.99777106478e-1) * s
    poly = (poly - 3.33329491539e-1) * s * r + r
    y = base + poly
    return jnp.where(x < 0.0, -y, y)


def rows_at(start, size):
    return pl.ds(pl.multiple_of(start, SUBLANES), size)


def kernel(
    plan,
    prior,
    terminal,
    perturbation,
    angles,
    out,
    x,
    z,
    noise,
    seen,
    gram,
    xy_in,
    part,
    z_in,
    numer,
    w,
    xb,
    send,
    recv,
    once_send,
    once_recv,
    local,
):
    n_space, n_mem, ny, nz, scatter_z, mixed, temper = plan
    nxy = (n_space // CORES) * ny
    chunks, rows, _ = gram.shape
    rows3 = rows // nxy
    samples = z.shape[0]
    members = prior.shape[0]
    variables = terminal.shape[1]
    lanes = numer.shape[3]

    sp = lax.axis_index("space")
    me = lax.axis_index("mem")
    core = lax.rem(sp, CORES)
    other = 1 - core
    xi = lax.div(sp, CORES)
    yi = lax.rem(me, ny)
    zi = lax.div(me, ny)

    core_dev = (xi * CORES + other, me)

    nx = n_space // CORES
    nlow = ny if mixed else nz
    here = {"x": xi, "y": yi, "low": lax.rem(zi, nlow), "high": lax.div(zi, nlow)}
    size = {"x": nx, "y": ny, "low": nlow, "high": nz // nlow}

    def position(axes):
        return here[axes[0]] * size[axes[1]] + here[axes[1]]

    def peer(axes, d):
        p = lax.rem(position(axes) + d, size[axes[0]] * size[axes[1]])
        at = dict(here)
        at[axes[0]] = lax.div(p, size[axes[1]])
        at[axes[1]] = lax.rem(p, size[axes[1]])
        return p, (at["x"] * CORES + core, (at["high"] * nlow + at["low"]) * ny + at["y"])

    orders = [(("x", "y"), ("high", "low"))]
    if mixed:
        orders += [orders[0], (("x", "low"), ("high", "y")), (("y", "low"), ("high", "x"))]
    orders = [orders[c % len(orders)] for c in range(chunks)]

    def mem_peer(d):
        p = lax.rem(me + d, n_mem)
        return p, (sp, p)

    def cols(p):
        return pl.ds(pl.multiple_of(p * variables, variables), variables)

    mine = cols(core)
    my_samples = rows_at(core * samples, samples)
    its_samples = rows_at(other * samples, samples)
    my_members = rows_at(me * members, members)

    loads = [
        pltpu.make_async_copy(
            prior.at[:, cols(me)], x.at[my_members, mine], local.at[0]
        ),
        pltpu.make_async_copy(terminal.at[my_samples, :], z.at[:, mine], local.at[1]),
        pltpu.make_async_copy(angles, seen.at[:, mine], local.at[2]),
        pltpu.make_async_copy(
            perturbation.at[:, my_samples, :], noise.at[:, :, mine], local.at[3]
        ),
    ]
    for copy in loads:
        copy.start()

    barrier = pltpu.get_barrier_semaphore()
    greet = [core_dev]
    for axes in sorted({axes for order in orders for axes in order}):
        n = size[axes[0]] * size[axes[1]]
        greet += [peer(axes, d)[1] for d in range(1, n)]
    greet += [mem_peer(d)[1] for d in range(1, n_mem)]
    for dev in greet:
        pl.semaphore_signal(barrier, inc=1, device_id=dev, device_id_type=MESH)
    pl.semaphore_wait(barrier, len(greet))

    def put_once(src, dst, i, dev):
        copy = pltpu.make_async_remote_copy(
            src_ref=src,
            dst_ref=dst,
            send_sem=once_send.at[i],
            recv_sem=once_recv.at[i],
            device_id=dev,
            device_id_type=MESH,
        )
        copy.start()
        return copy

    exchange = []
    for d in range(1, n_mem):
        p, dev = mem_peer(d)
        exchange.append(put_once(prior.at[:, cols(p)], x.at[my_members, mine], d - 1, dev))
    i = n_mem - 1
    swaps = [
        put_once(terminal.at[its_samples, :], z.at[:, mine], i, core_dev),
        put_once(angles, seen.at[:, mine], i + 1, core_dev),
        put_once(prior.at[:, cols(me)], x.at[my_members, mine], i + 2, core_dev),
        put_once(perturbation.at[:, its_samples, :], noise.at[:, :, mine], i + 3, core_dev),
    ]
    i = i + 4
    for d, copy in enumerate(exchange):
        copy.wait_recv()
        theirs = rows_at(lax.rem(me + n_mem - d - 1, n_mem) * members, members)
        swaps.append(put_once(x.at[theirs, mine], x.at[theirs, mine], i + d, core_dev))
    i = i + n_mem - 1
    for copy in loads:
        copy.wait()
    for copy in swaps:
        copy.wait_recv()

    xs = x[...]
    for j, piece in enumerate(split(xs, 3)):
        xb[j] = piece
    norms = jnp.zeros((SUBLANES, xs.shape[0]), jnp.float32)
    for piece in reversed(split(xs * xs, 3)):
        norms = norms + lax.dot_general(
            jnp.ones((SUBLANES, xs.shape[1]), jnp.bfloat16),
            piece,
            (((1,), (1,)), ((), ())),
            preferred_element_type=jnp.float32,
        )
    norms = norms[:1]

    first_z = nxy - 1
    first_gz = first_z + nz - 1
    first_gxy = first_gz + nz - 1

    def chunk(c):
        where = pl.ds(c * rows, rows)
        first, second = orders[c]
        mine_xy = rows_at(position(first) * rows3, rows3)
        z_at = position(second)
        for k in range(ITERS):
            t = 1.0 - k / ITERS
            dt = 1.0 / ITERS
            alpha = 1.0 - 0.5 * t
            drift = -0.5 / alpha
            g2 = 1.0 + t / alpha
            damp = 1.0 - t
            started = []

            def put(src, dst, i, dev):
                copy = pltpu.make_async_remote_copy(
                    src_ref=src,
                    dst_ref=dst,
                    send_sem=send.at[k % 2, c, i],
                    recv_sem=recv.at[k % 2, c, i],
                    device_id=dev,
                    device_id_type=MESH,
                )
                copy.start()
                started.append(copy)
                return copy

            gram[c] = 2.0 * alpha * product(z[where, :], [xb[0], xb[1], xb[2]], 1) - alpha * alpha * norms
            group = []
            for d in range(1, nxy):
                p, dev = peer(first, d)
                group.append(
                    put(gram.at[c, rows_at(p * rows3, rows3), :], xy_in.at[c, d - 1], d - 1, dev)
                )
            yield
            total = gram[c, mine_xy, :]
            for d, copy in enumerate(group):
                copy.wait_recv()
                total = total + xy_in[c, d]
            group = []
            if scatter_z:
                for p in range(nz):
                    part[c, p] = total[:, p * lanes : (p + 1) * lanes]
            else:
                part[c, 0] = total
            for d in range(1, nz):
                p, dev = peer(second, d)
                src = part.at[c, p] if scatter_z else part.at[c, 0]
                group.append(put(src, z_in.at[k % 2, c, d - 1], first_z + d - 1, dev))
            yield
            block = part[c, z_at] if scatter_z else part[c, 0]
            for d, copy in enumerate(group):
                copy.wait_recv()
                block = block + z_in[k % 2, c, d]
            if scatter_z:
                numer[c, z_at] = block
                group = [
                    put(numer.at[c, z_at], numer.at[c, z_at], first_gz + d - 1, peer(second, d)[1])
                    for d in range(1, nz)
                ]
                yield
                for copy in group:
                    copy.wait_recv()
                block = jnp.concatenate([numer[c, p] for p in range(nz)], axis=1)
            logits = block / (2.0 * t * temper)
            e = jnp.exp(logits - jnp.max(logits, axis=1, keepdims=True))
            w[c, mine_xy, :] = e / jnp.sum(e, axis=1, keepdims=True)
            group = [
                put(w.at[c, mine_xy, :], w.at[c, mine_xy, :], first_gxy + d - 1, peer(first, d)[1])
                for d in range(1, nxy)
            ]
            yield
            for copy in group:
                copy.wait_recv()
            blend = product(w[c], [xb[0], xb[1]], 0)
            zs = z[where, :]
            score = -(zs - alpha * blend) / t + damp * 4.0 * (seen[...] - arctan(zs)) / (
                1.0 + zs * zs
            )
            z[where, :] = (
                zs + dt * (-drift * zs + g2 * score) + math.sqrt(dt * g2) * noise[k, where, :]
            )
            for copy in started:
                copy.wait_send()
        target = out.at[rows_at(core * samples + c * rows, rows), :]
        result = pltpu.make_async_copy(z.at[where, mine], target, local.at[4 + c])
        result.start()
        swap = put_once(z.at[where, cols(other)], target, i + c, core_dev)
        yield
        result.wait()
        swap.wait()

    running = [chunk(c) for c in range(chunks)]
    while running:
        still = []
        for item in running:
            try:
                next(item)
                still.append(item)
            except StopIteration:
                pass
        running = still
    for copy in exchange + swaps:
        copy.wait_send()


def per_device(prior, terminal, perturbation, angles):
    n_space, n_mem = lax.axis_size("space"), lax.axis_size("mem")
    samples, variables = terminal.shape
    members = prior.shape[0] * n_mem
    nx = n_space // CORES
    ny = math.gcd(nx, n_mem)
    nz = n_mem // ny
    nxy = nx * ny
    half = samples // CORES
    chunks = CHUNKS
    while chunks > 1 and half % (chunks * nxy * SUBLANES):
        chunks //= 2
    rows = half // chunks
    rows3 = rows // nxy
    scatter_z = members % (nz * LANES) == 0
    pieces = nz if scatter_z else 1
    lanes = members // pieces
    mixed = chunks == CHUNKS and nx == ny and nz % ny == 0
    temper = math.sqrt(variables * n_space * n_mem)
    f32 = jnp.float32
    exchanges = 2 * (nxy - 1 + nz - 1)
    once = 2 * (n_mem - 1) + 4 + chunks
    iters = perturbation.shape[0]
    anywhere = pl.BlockSpec(memory_space=pl.ANY)
    return pl.pallas_call(
        functools.partial(kernel, (n_space, n_mem, ny, nz, scatter_z, mixed, temper)),
        out_shape=jax.ShapeDtypeStruct((samples, variables), f32),
        in_specs=[anywhere] * 4,
        out_specs=anywhere,
        scratch_shapes=[
            pltpu.VMEM((members, CORES * variables), f32),
            pltpu.VMEM((half, CORES * variables), f32),
            pltpu.VMEM((iters, half, CORES * variables), f32),
            pltpu.VMEM((1, CORES * variables), f32),
            pltpu.VMEM((chunks, rows, members), f32),
            pltpu.VMEM((chunks, nxy - 1, rows3, members), f32),
            pltpu.VMEM((chunks, pieces, rows3, lanes), f32),
            pltpu.VMEM((2, chunks, nz - 1, rows3, lanes), f32),
            pltpu.VMEM((chunks, pieces, rows3, lanes), f32),
            pltpu.VMEM((chunks, rows, members), f32),
            pltpu.VMEM((3, members, CORES * variables), jnp.bfloat16),
            pltpu.SemaphoreType.DMA((2, chunks, exchanges)),
            pltpu.SemaphoreType.DMA((2, chunks, exchanges)),
            pltpu.SemaphoreType.DMA((once,)),
            pltpu.SemaphoreType.DMA((once,)),
            pltpu.SemaphoreType.DMA((4 + chunks,)),
        ],
        compiler_params=pltpu.CompilerParams(collective_id=0, has_side_effects=True),
    )(prior, terminal, perturbation, angles.reshape(1, variables))


def solution(mesh):
    in_specs = (
        P("mem", "space"),
        P(None, ("space", "mem")),
        P(None, None, ("space", "mem")),
        P(("space", "mem")),
    )
    out_specs = P(None, ("space", "mem"))
    return jax.shard_map(
        per_device, mesh=mesh, in_specs=in_specs, out_specs=out_specs, check_vma=False
    )
```

```python
import functools
import math

import jax
import jax.numpy as jnp
from jax import lax
from jax.experimental import pallas as pl
from jax.experimental.pallas import tpu as pltpu
from jax.sharding import PartitionSpec as P

ITERS = 3
CHUNKS = 4
CORES = 2
SUBLANES = 8
LANES = 128
MESH = pl.DeviceIdType.MESH


def split(a, parts):
    out = []
    for _ in range(parts):
        out.append(a.astype(jnp.bfloat16))
        a = a - out[-1].astype(jnp.float32)
    return out


def product(a, parts, contract_b):
    n = a.shape[0]
    lhs = split(a, len(parts))
    total = None
    for i in reversed(range(len(parts))):
        rows = lhs[: len(parts) - i]
        both = lax.dot_general(
            jnp.concatenate(rows, axis=0),
            parts[i],
            (((1,), (contract_b,)), ((), ())),
            preferred_element_type=jnp.float32,
        )
        for j in reversed(range(len(rows))):
            term = both[j * n : (j + 1) * n]
            total = term if total is None else total + term
    return total


def arctan(x):
    a = jnp.abs(x)
    big = a > 2.414213562373095
    mid = a > 0.4142135623730950
    num = jnp.where(big, -1.0, jnp.where(mid, a - 1.0, a))
    den = jnp.where(big, a, jnp.where(mid, a + 1.0, 1.0))
    base = jnp.where(big, math.pi / 2, jnp.where(mid, math.pi / 4, 0.0))
    r = num / den
    s = r * r
    poly = ((8.05374449538e-2 * s - 1.38776856032e-1) * s + 1.99777106478e-1) * s
    poly = (poly - 3.33329491539e-1) * s * r + r
    y = base + poly
    return jnp.where(x < 0.0, -y, y)


def rows_at(start, size):
    return pl.ds(pl.multiple_of(start, SUBLANES), size)


def kernel(
    plan,
    prior,
    terminal,
    perturbation,
    angles,
    out,
    x,
    z,
    noise,
    seen,
    gram,
    xy_in,
    part,
    z_in,
    numer,
    w,
    xb,
    send,
    recv,
    once_send,
    once_recv,
    local,
):
    n_space, n_mem, ny, nz, scatter_z, mixed, temper = plan
    nxy = (n_space // CORES) * ny
    chunks, rows, _ = gram.shape
    rows3 = rows // nxy
    samples = z.shape[0]
    members = prior.shape[0]
    variables = terminal.shape[1]
    lanes = numer.shape[3]

    sp = lax.axis_index("space")
    me = lax.axis_index("mem")
    core = lax.rem(sp, CORES)
    other = 1 - core
    xi = lax.div(sp, CORES)
    yi = lax.rem(me, ny)
    zi = lax.div(me, ny)

    core_dev = (xi * CORES + other, me)

    here = {"x": xi, "y": yi, "z": zi, "one": 0}
    size = {"x": n_space // CORES, "y": ny, "z": nz, "one": 1}

    def position(axes):
        return here[axes[0]] * size[axes[1]] + here[axes[1]]

    def peer(axes, d):
        p = lax.rem(position(axes) + d, size[axes[0]] * size[axes[1]])
        at = dict(here)
        at[axes[0]] = lax.div(p, size[axes[1]])
        at[axes[1]] = lax.rem(p, size[axes[1]])
        return p, (at["x"] * CORES + core, at["z"] * ny + at["y"])

    orders = [(("x", "y"), ("one", "z"))]
    if mixed:
        orders += [orders[0][::-1], orders[0], orders[0]]
    orders = [orders[c % len(orders)] for c in range(chunks)]

    def mem_peer(d):
        p = lax.rem(me + d, n_mem)
        return p, (sp, p)

    def cols(p):
        return pl.ds(pl.multiple_of(p * variables, variables), variables)

    mine = cols(core)
    my_samples = rows_at(core * samples, samples)
    its_samples = rows_at(other * samples, samples)
    my_members = rows_at(me * members, members)

    loads = [
        pltpu.make_async_copy(
            prior.at[:, cols(me)], x.at[my_members, mine], local.at[0]
        ),
        pltpu.make_async_copy(terminal.at[my_samples, :], z.at[:, mine], local.at[1]),
        pltpu.make_async_copy(angles, seen.at[:, mine], local.at[2]),
        pltpu.make_async_copy(
            perturbation.at[:, my_samples, :], noise.at[:, :, mine], local.at[3]
        ),
    ]
    for copy in loads:
        copy.start()

    barrier = pltpu.get_barrier_semaphore()
    greet = [core_dev]
    for axes in sorted({axes for order in orders for axes in order}):
        n = size[axes[0]] * size[axes[1]]
        greet += [peer(axes, d)[1] for d in range(1, n)]
    greet += [mem_peer(d)[1] for d in range(1, n_mem)]
    for dev in greet:
        pl.semaphore_signal(barrier, inc=1, device_id=dev, device_id_type=MESH)
    pl.semaphore_wait(barrier, len(greet))

    def put_once(src, dst, i, dev):
        copy = pltpu.make_async_remote_copy(
            src_ref=src,
            dst_ref=dst,
            send_sem=once_send.at[i],
            recv_sem=once_recv.at[i],
            device_id=dev,
            device_id_type=MESH,
        )
        copy.start()
        return copy

    exchange = []
    for d in range(1, n_mem):
        p, dev = mem_peer(d)
        exchange.append(put_once(prior.at[:, cols(p)], x.at[my_members, mine], d - 1, dev))
    i = n_mem - 1
    swaps = [
        put_once(terminal.at[its_samples, :], z.at[:, mine], i, core_dev),
        put_once(angles, seen.at[:, mine], i + 1, core_dev),
        put_once(prior.at[:, cols(me)], x.at[my_members, mine], i + 2, core_dev),
        put_once(perturbation.at[:, its_samples, :], noise.at[:, :, mine], i + 3, core_dev),
    ]
    i = i + 4
    for d, copy in enumerate(exchange):
        copy.wait_recv()
        theirs = rows_at(lax.rem(me + n_mem - d - 1, n_mem) * members, members)
        swaps.append(put_once(x.at[theirs, mine], x.at[theirs, mine], i + d, core_dev))
    i = i + n_mem - 1
    for copy in loads:
        copy.wait()
    for copy in swaps:
        copy.wait_recv()

    xs = x[...]
    for j, piece in enumerate(split(xs, 3)):
        xb[j] = piece
    norms = jnp.zeros((SUBLANES, xs.shape[0]), jnp.float32)
    for piece in reversed(split(xs * xs, 3)):
        norms = norms + lax.dot_general(
            jnp.ones((SUBLANES, xs.shape[1]), jnp.bfloat16),
            piece,
            (((1,), (1,)), ((), ())),
            preferred_element_type=jnp.float32,
        )
    norms = norms[:1]

    first_z = nxy - 1
    first_gz = first_z + nz - 1
    first_gxy = first_gz + nz - 1

    def chunk(c):
        where = pl.ds(c * rows, rows)
        first, second = orders[c]
        mine_xy = rows_at(position(first) * rows3, rows3)
        z_at = position(second)
        for k in range(ITERS):
            t = 1.0 - k / ITERS
            dt = 1.0 / ITERS
            alpha = 1.0 - 0.5 * t
            drift = -0.5 / alpha
            g2 = 1.0 + t / alpha
            damp = 1.0 - t
            started = []

            def put(src, dst, i, dev):
                copy = pltpu.make_async_remote_copy(
                    src_ref=src,
                    dst_ref=dst,
                    send_sem=send.at[k % 2, c, i],
                    recv_sem=recv.at[k % 2, c, i],
                    device_id=dev,
                    device_id_type=MESH,
                )
                copy.start()
                started.append(copy)
                return copy

            gram[c] = 2.0 * alpha * product(z[where, :], [xb[0], xb[1], xb[2]], 1) - alpha * alpha * norms
            group = []
            for d in range(1, nxy):
                p, dev = peer(first, d)
                group.append(
                    put(gram.at[c, rows_at(p * rows3, rows3), :], xy_in.at[c, d - 1], d - 1, dev)
                )
            yield
            total = gram[c, mine_xy, :]
            for d, copy in enumerate(group):
                copy.wait_recv()
                total = total + xy_in[c, d]
            group = []
            if scatter_z:
                for p in range(nz):
                    part[c, p] = total[:, p * lanes : (p + 1) * lanes]
            else:
                part[c, 0] = total
            for d in range(1, nz):
                p, dev = peer(second, d)
                src = part.at[c, p] if scatter_z else part.at[c, 0]
                group.append(put(src, z_in.at[k % 2, c, d - 1], first_z + d - 1, dev))
            yield
            block = part[c, z_at] if scatter_z else part[c, 0]
            for d, copy in enumerate(group):
                copy.wait_recv()
                block = block + z_in[k % 2, c, d]
            if scatter_z:
                numer[c, z_at] = block
                group = [
                    put(numer.at[c, z_at], numer.at[c, z_at], first_gz + d - 1, peer(second, d)[1])
                    for d in range(1, nz)
                ]
                yield
                for copy in group:
                    copy.wait_recv()
                block = jnp.concatenate([numer[c, p] for p in range(nz)], axis=1)
            logits = block / (2.0 * t * temper)
            e = jnp.exp(logits - jnp.max(logits, axis=1, keepdims=True))
            w[c, mine_xy, :] = e / jnp.sum(e, axis=1, keepdims=True)
            group = [
                put(w.at[c, mine_xy, :], w.at[c, mine_xy, :], first_gxy + d - 1, peer(first, d)[1])
                for d in range(1, nxy)
            ]
            yield
            for copy in group:
                copy.wait_recv()
            blend = product(w[c], [xb[0], xb[1]], 0)
            zs = z[where, :]
            score = -(zs - alpha * blend) / t + damp * 4.0 * (seen[...] - arctan(zs)) / (
                1.0 + zs * zs
            )
            z[where, :] = (
                zs + dt * (-drift * zs + g2 * score) + math.sqrt(dt * g2) * noise[k, where, :]
            )
            for copy in started:
                copy.wait_send()
        target = out.at[rows_at(core * samples + c * rows, rows), :]
        result = pltpu.make_async_copy(z.at[where, mine], target, local.at[4 + c])
        result.start()
        swap = put_once(z.at[where, cols(other)], target, i + c, core_dev)
        yield
        result.wait()
        swap.wait()

    running = [chunk(c) for c in range(chunks)]
    while running:
        still = []
        for item in running:
            try:
                next(item)
                still.append(item)
            except StopIteration:
                pass
        running = still
    for copy in exchange + swaps:
        copy.wait_send()


def per_device(prior, terminal, perturbation, angles):
    n_space, n_mem = lax.axis_size("space"), lax.axis_size("mem")
    samples, variables = terminal.shape
    members = prior.shape[0] * n_mem
    nx = n_space // CORES
    ny = math.gcd(nx, n_mem)
    nz = n_mem // ny
    nxy = nx * ny
    half = samples // CORES
    chunks = CHUNKS
    while chunks > 1 and half % (chunks * nxy * SUBLANES):
        chunks //= 2
    rows = half // chunks
    rows3 = rows // nxy
    scatter_z = members % (nz * LANES) == 0
    pieces = nz if scatter_z else 1
    lanes = members // pieces
    mixed = nxy == nz and scatter_z
    temper = math.sqrt(variables * n_space * n_mem)
    f32 = jnp.float32
    exchanges = 2 * (nxy - 1 + nz - 1)
    once = 2 * (n_mem - 1) + 4 + chunks
    iters = perturbation.shape[0]
    anywhere = pl.BlockSpec(memory_space=pl.ANY)
    return pl.pallas_call(
        functools.partial(kernel, (n_space, n_mem, ny, nz, scatter_z, mixed, temper)),
        out_shape=jax.ShapeDtypeStruct((samples, variables), f32),
        in_specs=[anywhere] * 4,
        out_specs=anywhere,
        scratch_shapes=[
            pltpu.VMEM((members, CORES * variables), f32),
            pltpu.VMEM((half, CORES * variables), f32),
            pltpu.VMEM((iters, half, CORES * variables), f32),
            pltpu.VMEM((1, CORES * variables), f32),
            pltpu.VMEM((chunks, rows, members), f32),
            pltpu.VMEM((chunks, nxy - 1, rows3, members), f32),
            pltpu.VMEM((chunks, pieces, rows3, lanes), f32),
            pltpu.VMEM((2, chunks, nz - 1, rows3, lanes), f32),
            pltpu.VMEM((chunks, pieces, rows3, lanes), f32),
            pltpu.VMEM((chunks, rows, members), f32),
            pltpu.VMEM((3, members, CORES * variables), jnp.bfloat16),
            pltpu.SemaphoreType.DMA((2, chunks, exchanges)),
            pltpu.SemaphoreType.DMA((2, chunks, exchanges)),
            pltpu.SemaphoreType.DMA((once,)),
            pltpu.SemaphoreType.DMA((once,)),
            pltpu.SemaphoreType.DMA((4 + chunks,)),
        ],
        compiler_params=pltpu.CompilerParams(collective_id=0, has_side_effects=True),
    )(prior, terminal, perturbation, angles.reshape(1, variables))


def solution(mesh):
    in_specs = (
        P("mem", "space"),
        P(None, ("space", "mem")),
        P(None, None, ("space", "mem")),
        P(("space", "mem")),
    )
    out_specs = P(None, ("space", "mem"))
    return jax.shard_map(
        per_device, mesh=mesh, in_specs=in_specs, out_specs=out_specs, check_vma=False
    )
```
